512 devices in a mesh: energy: 32 (over z, core), seg: 16 (over y, x).
Axes of the slice: x: 4, y: 4, z: 16, core: 2. Of those that a mesh axis runs over, the one named last changes fastest.
Arguments:
- energies: float32 [32], P('energy'), may hold values from -2 to 2
- h_blocks: float32 [16, 4, 64, 128], P('seg'), as said below
- couplings: float32 [16, 4, 64, 128], P('seg')
- shift_real: float32 [32, 16, 256], P('energy', 'seg'), may hold values from -0.625 to 0.625
- shift_rate: float32 [32, 16, 256], P('energy', 'seg'), may hold values from 0.005 to 0.05
- screened: float32 [8, 16, 4, 64, 128], P(None, 'seg'), may hold values from -3 to 3
- sources: int32 [32, 8], P('energy'), may hold values from 0 to 31, as said below
- counts: int32 [16], P('seg'), may hold values from 1 to 4, 32 in all
Outputs:
- sigma_new: float32 [32, 16, 4, 64, 128], P('energy', 'seg')
The draws below stay inside these ranges and needn't reach their ends.
Inputs may be any that keep to these rules, and one draw needn't show every extreme that they name: `h_blocks`: each diagonal block is Hermitian: its real part symmetric, its imaginary part antisymmetric. The counts sum to 32; some segment holds exactly 4 blocks. For every group of 1 consecutive energies starting at a multiple of 1, its 8 sources lie at most 1 in any one such group, and exactly 1 in some group.
All inputs are finite; a program needn't handle non-finite values.
Results may differ from the reference program's by a relative error of at most 0.0029.
Values may be sent and summed in bfloat16 or wider, within the bound.
A program may use at most 64 MiB of HBM per device.

```python
import math
import jax
import jax.numpy as jnp
import numpy as np
from jax import lax

BS = 64
MAXB = 4
NSHIFT = 8
E_DEV = 1
SEGS = 16
ENERGIES = 32
PULL = 1


def hermitian_from(real_draw, imag_draw, factor):
    real_part = (real_draw + jnp.swapaxes(real_draw, -1, -2)) * (0.5 * factor)
    imag_part = (imag_draw - jnp.swapaxes(imag_draw, -1, -2)) * (0.5 * factor)
    return jnp.concatenate([real_part, imag_part], -1)


def draw_h_blocks(key, part):
    keys = jax.random.split(jax.random.fold_in(key, 11), 4)
    common_shape = (BS, BS)
    spread_shape = (SEGS, MAXB, BS, BS)
    common_real = jax.random.normal(keys[0], common_shape, jnp.float32)
    common_imag = jax.random.normal(keys[1], common_shape, jnp.float32)
    spread_real = jax.random.normal(keys[2], spread_shape, jnp.float32)
    spread_imag = jax.random.normal(keys[3], spread_shape, jnp.float32)
    common = hermitian_from(common_real, common_imag, 0.75 / math.sqrt(BS))
    spread = hermitian_from(spread_real, spread_imag, 0.1 / math.sqrt(BS))
    return common[None, None] + spread


def draw_couplings(key, part):
    common_key, spread_key = jax.random.split(jax.random.fold_in(key, 13))
    common = jax.random.normal(common_key, (BS, 2 * BS), jnp.float32)
    spread = jax.random.normal(spread_key, (SEGS, MAXB, BS, 2 * BS), jnp.float32)
    return common[None, None] * (0.32 / math.sqrt(BS)) + spread * (0.035 / math.sqrt(BS))


def shuffled_slots(row_key):
    groups = ENERGIES // E_DEV
    return jax.random.permutation(row_key, groups * PULL)


def draw_sources(key, part):
    order_key, pick_key = jax.random.split(jax.random.fold_in(key, 17))
    groups = ENERGIES // E_DEV
    requests = E_DEV * NSHIFT
    row_keys = jax.random.split(order_key, groups)
    slots = jax.vmap(shuffled_slots)(row_keys)[:, :requests]
    owner_of = slots % groups
    within = jax.random.randint(pick_key, (groups, requests), 0, E_DEV)
    return (owner_of * E_DEV + within).astype(jnp.int32).reshape(ENERGIES, NSHIFT)


def level_of(key, extent, shards, low, largest):
    def one(dim, blocks):
        steps = jax.random.uniform(jax.random.fold_in(jax.random.fold_in(key, 6), dim), (blocks,), jnp.float32, low / len(shards), largest / len(shards))
        return jnp.repeat(jnp.exp(steps), extent[dim] // blocks).reshape((-1,) + (1,) * (len(extent) - dim - 1))

    factor_of = one(*shards[0])
    for cut in shards[1:]:
        factor_of = factor_of * one(*cut)
    return factor_of


def split_up(number_of, total, reach, lean):
    loads = [(1 << 20) // math.isqrt(grade ** lean) + 1 for grade in range(2, number_of + 1)]
    surplus, given = total - reach - (number_of - 1), [1] * (number_of - 1)
    while surplus > 0:
        candidates = [i for i in range(number_of - 1) if given[i] < reach]
        pool, budget = sum([loads[i] for i in candidates]), surplus
        for i in candidates:
            more = min(reach - given[i], max(1, budget * loads[i] // pool), surplus)
            given[i] = given[i] + more
            surplus = surplus - more
    return np.array([reach] + given)


def ragged(key, amount, total, limit, lean):
    if amount == 2:
        one = jax.random.randint(key, (), max(1, total - limit), min(limit, total - 1) + 1)
        return jnp.stack([one, total - one])
    tallies = jnp.asarray(split_up(amount, total, limit, lean), jnp.int32)
    pairs = (amount - 1) // 2
    giver, receiver = tallies[1:1 + 2 * pairs:2], tallies[2:2 + 2 * pairs:2]
    margin = jnp.minimum(giver - 1, limit - receiver)
    moved = jax.random.randint(jax.random.fold_in(key, 1), (pairs,), 0, 1 << 20) % (margin + 1)
    tallies = tallies.at[1:1 + 2 * pairs:2].set(giver - moved).at[2:2 + 2 * pairs:2].set(receiver + moved)
    return tallies[jax.random.permutation(jax.random.fold_in(key, 2), amount)]


def gaussian(rng, extent, scale, limit, shards=(), kind=jnp.bfloat16):
    entries = jax.random.normal(rng, extent, jnp.float32) * scale
    if len(shards) > 0:
        entries = level_of(rng, extent, shards, -0.22, 0.18) * entries
    return jnp.clip(entries, min=-limit, max=limit).astype(kind)


def setup_inputs(seed: int = 0) -> dict:
    key_list = jax.random.split(jax.random.key(seed), 9)
    return {
        "energies": jnp.clip(jax.random.uniform(key_list[0], (ENERGIES,), jnp.float32, -2.0, 2.0) * level_of(key_list[0], (ENERGIES,), ((0, 32),), -0.4, 0.0), -2.0, 2.0),
        "h_blocks": draw_h_blocks(jax.random.fold_in(key_list[8], 71), 0),
        "couplings": draw_couplings(jax.random.fold_in(key_list[8], 71), 0),
        "shift_real": gaussian(key_list[3], (ENERGIES, SEGS, MAXB * BS), 0.1, 0.625, ((0, 32), (1, 16)), jnp.float32),
        "shift_rate": jnp.clip(jnp.exp(math.log(0.05) - 2.3025851 * jax.random.uniform(key_list[4], (ENERGIES, SEGS, MAXB * BS), jnp.float32) ** level_of(key_list[4], (ENERGIES, SEGS, MAXB * BS), ((0, 32), (1, 16)), -0.2, 0.2)), 0.005, 0.05),
        "screened": gaussian(key_list[5], (NSHIFT, SEGS, MAXB, BS, 2 * BS), 0.5, 3.0, ((1, 16),), jnp.float32),
        "sources": draw_sources(jax.random.fold_in(key_list[8], 71), 0),
        "counts": ragged(key_list[7], SEGS, 2 * SEGS, MAXB, 2).astype(jnp.int32),
    }


broadening = 0.02

def expand(matrix):
    order = matrix.shape[-2]
    real_part = matrix[..., :order]
    imag_part = matrix[..., order:]
    return jnp.concatenate([jnp.concatenate([real_part, imag_part], -1), jnp.concatenate([-imag_part, real_part], -1)], -2)

def complex_product(matrix, other):
    return jnp.matmul(matrix, expand(other), precision=lax.Precision.HIGHEST)

def adjoint(matrix):
    order = matrix.shape[-2]
    return jnp.concatenate([jnp.swapaxes(matrix[..., :order], -1, -2), -jnp.swapaxes(matrix[..., order:], -1, -2)], -1)

def complex_inverse(matrix):
    order = matrix.shape[-2]
    real_part = matrix[..., :order]
    imag_part = matrix[..., order:]
    real_form = jnp.concatenate([jnp.concatenate([real_part, -imag_part], -1), jnp.concatenate([imag_part, real_part], -1)], -2)
    flipped = jnp.swapaxes(real_form, -1, -2)
    normal = jnp.matmul(flipped, real_form, precision=lax.Precision.HIGHEST)
    factor = jnp.linalg.cholesky(normal)
    middle = jax.scipy.linalg.solve_triangular(factor, flipped[..., :order], lower=True)
    solved = jax.scipy.linalg.solve_triangular(factor, middle, lower=True, trans=1)
    return jnp.concatenate([solved[..., :order, :], solved[..., order:, :]], -1)

def unit_block(order):
    return jnp.concatenate([jnp.eye(order, dtype=jnp.float32), jnp.zeros((order, order), jnp.float32)], -1)

def entry_product(green, weight):
    order = green.shape[-2]
    green_re = green[..., :order]
    green_im = green[..., order:]
    weight_re = weight[..., :order]
    weight_im = weight[..., order:]
    return jnp.concatenate([green_re * weight_re - green_im * weight_im, green_re * weight_im + green_im * weight_re], -1)

def build_blocks(energies, hams, shift_real, shift_rate):
    slots, order = (hams.shape[0], hams.shape[1])
    batch = energies.shape[0]
    identity = jnp.eye(order, dtype=jnp.float32)
    shifts = shift_real.reshape(batch, slots, order)
    rates = shift_rate.reshape(batch, slots, order)
    real_part = energies[:, None, None, None] * identity - hams[None, :, :, :order] - shifts[..., :, None] * identity
    imag_part = broadening * identity - hams[None, :, :, order:] + rates[..., :, None] * identity
    return jnp.concatenate([real_part, imag_part], -1)

def segment_summary(diag_a, links, used_blocks):
    slots = diag_a.shape[1]
    last_block = complex_inverse(diag_a[:, 0])
    head_block, upper_block, lower_block = (last_block, last_block, last_block)
    for k in range(1, slots):
        link_block = links[k]
        back_link = adjoint(link_block)
        fresh_block = complex_inverse(diag_a[:, k] - complex_product(complex_product(back_link, last_block), link_block))
        left_part = complex_product(upper_block, link_block)
        right_part = complex_product(back_link, lower_block)
        new_upper = complex_product(left_part, fresh_block)
        new_lower = complex_product(fresh_block, right_part)
        new_head = head_block + complex_product(new_upper, right_part)
        live = k < used_blocks
        head_block = jnp.where(live, new_head, head_block)
        upper_block = jnp.where(live, new_upper, upper_block)
        lower_block = jnp.where(live, new_lower, lower_block)
        last_block = jnp.where(live, fresh_block, last_block)
    return (head_block, upper_block, lower_block, last_block)

def pick_blocks(flag, first_item, second_item):
    return jnp.where(flag[..., None, None] > 0.5, first_item, second_item)

def join_segments(left_group, right_group):
    a, b, c, d, entry_a, flag_a = left_group
    p, q, r, s, link_v, flag_b = right_group
    back_v = adjoint(link_v)
    order = a.shape[-2]
    cross_term = complex_product(complex_product(back_v, d), link_v)
    resolvent = complex_inverse(unit_block(order) - complex_product(p, cross_term))
    res_first = complex_product(resolvent, p)
    res_upper = complex_product(resolvent, q)
    d_link = complex_product(d, link_v)
    back_c = complex_product(back_v, c)
    b_link = complex_product(b, link_v)
    head_block = a + complex_product(complex_product(b_link, res_first), back_c)
    upper_block = complex_product(b_link, res_upper)
    k_lower = c + complex_product(complex_product(d_link, res_first), back_c)
    lower_block = complex_product(r, complex_product(back_v, k_lower))
    last_block = s + complex_product(complex_product(r, cross_term), res_upper)
    joined = (head_block, upper_block, lower_block, last_block, entry_a)
    result = tuple((pick_blocks(flag_a, rb, pick_blocks(flag_b, lb, jb)) for lb, rb, jb in zip(left_group[:5], right_group[:5], joined)))
    return result + (flag_a * flag_b,)

def segment_greens(diag_a, links, used_blocks, previous, sig_right):
    slots = diag_a.shape[1]
    forward_blocks = []
    for k in range(slots):
        link_block = links[k]
        inner_block = diag_a[:, k] - complex_product(complex_product(adjoint(link_block), previous), link_block) - jnp.where(k == used_blocks - 1, sig_right, 0.0)
        fresh_block = complex_inverse(inner_block)
        forward_blocks.append(fresh_block)
        previous = fresh_block
    greens = list(forward_blocks)
    for k in range(slots - 2, -1, -1):
        link_block = links[k + 1]
        spread = complex_product(forward_blocks[k], link_block)
        updated = forward_blocks[k] + complex_product(complex_product(spread, greens[k + 1]), complex_product(adjoint(link_block), forward_blocks[k]))
        greens[k] = jnp.where(k <= used_blocks - 2, updated, forward_blocks[k])
    greens = [jnp.where(k < used_blocks, greens[k], 0.0) for k in range(slots)]
    return jnp.stack(greens, 1)

def reference(energies, h_blocks, couplings, shift_real, shift_rate, screened, sources, counts):
    diag_a = jax.vmap(build_blocks, in_axes=(None, 0, 1, 1))(energies, h_blocks, shift_real, shift_rate)
    summaries = jax.vmap(segment_summary)(diag_a, couplings, counts)
    batch = energies.shape[0]
    entry_links = jnp.broadcast_to(couplings[:, 0][:, None], (SEGS, batch) + couplings.shape[2:])
    items = summaries + (entry_links, jnp.zeros((SEGS, batch), jnp.float32))
    zero_block = jnp.zeros((batch,) + couplings.shape[2:], jnp.float32)
    identity_item = (zero_block, zero_block, zero_block, zero_block, zero_block, jnp.ones((batch,), jnp.float32))

    def forward(running, element):
        return (join_segments(running, element), running)

    def backward(running, element):
        return (join_segments(element, running), running)
    _, before = lax.scan(forward, identity_item, items)
    _, after = lax.scan(backward, identity_item, items, reverse=True)
    right_link = after[4]
    sig_right = complex_product(complex_product(right_link, after[0]), adjoint(right_link))
    greens = jax.vmap(segment_greens)(diag_a, couplings, counts, before[3], sig_right)
    packed = jnp.swapaxes(greens, 0, 1).astype(jnp.bfloat16)
    accumulated = jnp.zeros(packed.shape, jnp.float32)
    for j in range(NSHIFT):
        picked = packed[sources[:, j]].astype(jnp.float32)
        accumulated = accumulated + entry_product(picked, screened[j][None])
    return accumulated
```

```python
import functools

import jax
import jax.numpy as jnp
from jax import lax
from jax.experimental import pallas as pl
from jax.experimental.pallas import tpu as pltpu
from jax.sharding import PartitionSpec as P

BS = 64
SLOTS = 4
WIDE = 2 * BS
broadening = 0.02
f32 = jnp.float32
bf16 = jnp.bfloat16
MESH = pl.DeviceIdType.MESH


def times_i(m):
    lane = lax.broadcasted_iota(jnp.int32, m.shape, 1)
    turned = pltpu.roll(m, BS, 1)
    return jnp.where(lane < BS, -turned, turned)


def expand(m):
    return jnp.concatenate([m, times_i(m)], 0)


def products(lefts, rights):
    left = lefts[0] if len(lefts) == 1 else jnp.concatenate(lefts, 0)
    right = [expand(m) for m in rights]
    right = right[0] if len(right) == 1 else jnp.concatenate(right, 1)
    out = jnp.dot(left, right, precision=lax.Precision.HIGHEST, preferred_element_type=f32)
    return [
        [out[BS * i : BS * i + BS, WIDE * j : WIDE * j + WIDE] for j in range(len(rights))]
        for i in range(len(lefts))
    ]


def product(a, b):
    return products([a], [b])[0][0]


def adjoint(m):
    t = jnp.transpose(m)
    return jnp.concatenate([t[:BS], -t[BS:]], 1)


def inverses(mats):
    lane8 = lax.broadcasted_iota(jnp.int32, (8, WIDE), 1)
    row8 = lax.broadcasted_iota(jnp.int32, (8, WIDE), 0)
    lane = lax.broadcasted_iota(jnp.int32, (BS, WIDE), 1)
    mats = list(mats)
    for p in range(BS // 8):
        own = (lane8 & (BS - 1)) // 8 == p
        panel = (lane & (BS - 1)) // 8 == p
        for b, m in enumerate(mats):
            rows = m[8 * p : 8 * p + 8]
            col_re = [jnp.broadcast_to(m[:, 8 * p + k : 8 * p + k + 1], (BS, WIDE)) for k in range(8)]
            col_im = [
                jnp.broadcast_to(m[:, BS + 8 * p + k : BS + 8 * p + k + 1], (BS, WIDE)) for k in range(8)
            ]
            x = jnp.where(own, jnp.where(lane8 == row8 + 8 * p, 1.0, 0.0), rows)
            z = jnp.where(own, jnp.where(lane8 == row8 + (8 * p + BS), 1.0, 0.0), times_i(rows))
            c_re = [c[8 * p : 8 * p + 8] for c in col_re]
            c_im = [c[8 * p : 8 * p + 8] for c in col_im]
            for k in range(8):
                p_re = jnp.broadcast_to(c_re[k][k : k + 1], (8, WIDE))
                p_im = jnp.broadcast_to(c_im[k][k : k + 1], (8, WIDE))
                scale = 1.0 / (p_re * p_re + p_im * p_im)
                q_re, q_im = p_re * scale, -(p_im * scale)
                x_k = jnp.broadcast_to(x[k : k + 1], (8, WIDE))
                z_k = jnp.broadcast_to(z[k : k + 1], (8, WIDE))
                x_s, z_s = x_k * q_re + z_k * q_im, z_k * q_re - x_k * q_im
                m_re, m_im = c_re[k], c_im[k]
                pivot = row8 == k
                for j in range(k + 1, 8):
                    r_re = jnp.broadcast_to(c_re[j][k : k + 1], (8, WIDE))
                    r_im = jnp.broadcast_to(c_im[j][k : k + 1], (8, WIDE))
                    s_re, s_im = r_re * q_re - r_im * q_im, r_re * q_im + r_im * q_re
                    c_re[j] = jnp.where(pivot, s_re, c_re[j] - (m_re * s_re - m_im * s_im))
                    c_im[j] = jnp.where(pivot, s_im, c_im[j] - (m_re * s_im + m_im * s_re))
                x, z = (
                    jnp.where(pivot, x_s, x - (m_re * x_s + m_im * z_s)),
                    jnp.where(pivot, z_s, z - (m_re * z_s - m_im * x_s)),
                )
            total = None
            for k in range(8):
                term = col_re[k] * x[k : k + 1] + col_im[k] * z[k : k + 1]
                total = term if total is None else total + term
            rest = jnp.where(panel, 0.0, m) - total
            parts = [x if q == p else rest[8 * q : 8 * q + 8] for q in range(BS // 8)]
            mats[b] = jnp.concatenate(parts, 0)
    return mats


def kernel(
    n_energy, n_seg,
    counts, sources, energies, h_ref, u_ref, real_ref, rate_ref, screened_hbm,
    out_ref,
    a_all, w_all, v_all, keep, factors, state, outbox, from_left, from_right, half_in,
    g_out, g_in, gathered, screened, turned,
    load_sem, left_send, left_recv, right_send, right_recv, half_send, half_recv,
    g_send, g_recv, ring_send, ring_recv, pair_send, pair_recv,
):
    e = lax.axis_index("energy")
    s = lax.axis_index("seg")
    n_z = n_energy // 2
    core = e % 2
    up_e = (e + 2) % n_energy
    down_e = (e + n_energy - 2) % n_energy
    pair_e = e + 1 - 2 * core

    barrier = pltpu.get_barrier_semaphore()
    hops = []
    h = 1
    while h < n_seg:
        hops.append(h)
        h *= 2
    greeted = [(up_e, s), (down_e, s), (pair_e, s)]
    for h in hops[:-1]:
        greeted += [(e, (s + h) % n_seg), (e, (s + n_seg - h) % n_seg)]
    greeted.append((e, (s + n_seg // 2) % n_seg))
    for device in greeted:
        pl.semaphore_signal(barrier, inc=1, device_id=device, device_id_type=MESH)

    load = pltpu.make_async_copy(screened_hbm, screened, load_sem)
    load.start()

    count = counts[0]
    energy = energies[0]
    row = lax.broadcasted_iota(jnp.int32, (BS, WIDE), 0)
    lane = lax.broadcasted_iota(jnp.int32, (BS, WIDE), 1)
    diagonal = (lane & (BS - 1)) == row
    attached = jnp.where(s > 0, 1.0, 0.0).astype(f32)
    for k in range(SLOTS):
        real = energy - real_ref[0, :, BS * k : BS * k + BS]
        imag = broadening + rate_ref[0, :, BS * k : BS * k + BS]
        line = jnp.concatenate([real, imag], 1)
        a_all[k] = jnp.where(diagonal, line, 0.0) - h_ref[0, k]
        w = u_ref[0, k]
        if k == 0:
            w = w * attached
        w_all[k] = w
        v_all[k] = adjoint(w)

    slot = [jnp.maximum(count + (place - SLOTS), 0) for place in range(SLOTS)]
    a = [a_all[i] for i in slot]
    w = [w_all[i] for i in slot]
    v = [v_all[i] for i in slot]
    many = jnp.full((BS, WIDE), count, jnp.int32)
    has0, has1, has2 = many >= 4, many >= 3, many >= 2

    g0, g2 = inverses([a[0], a[2]])
    ((g0w1, g0v0),) = products([g0], [w[1], v[0]])
    ((g2w3, g2v2),) = products([g2], [w[3], v[2]])
    (u01, d0l), (d01, l10) = products([w[0], v[1]], [g0w1, g0v0])
    (u23, d2x), (d2r, l32) = products([w[2], v[3]], [g2w3, g2v2])
    d1 = a[1] - jnp.where(has0, d01, 0.0) - d2x
    ul1 = jnp.where(has0, u01, w[1])
    l1l = jnp.where(has0, l10, v[1])
    (g1,) = inverses([d1])
    ((b1r, b1l),) = products([g1], [u23, l1l])
    (u13, d1l), (d1r, l31) = products([ul1, l32], [b1r, b1l])
    u_own = jnp.where(has1, u13, jnp.where(has2, u23, w[3]))
    l_own = jnp.where(has1, l31, jnp.where(has2, l32, v[3]))
    sigma_left = jnp.where(has1, d1r, 0.0) + jnp.where(has2, d2r, 0.0)
    to_left = jnp.where(has0, d0l, 0.0) + jnp.where(has1, d1l, jnp.where(has2, d2x, 0.0))

    outbox[0, 1] = u_own
    outbox[0, 2] = l_own
    outbox[0, 3] = to_left
    keep[0] = a[3]
    keep[1] = u_own
    keep[2] = l_own
    pl.semaphore_wait(barrier, len(greeted))

    def right_copy(level, h):
        return pltpu.make_async_remote_copy(
            src_ref=outbox.at[level, pl.ds(0, 3)],
            dst_ref=from_left.at[level],
            send_sem=right_send.at[level],
            recv_sem=left_recv.at[level],
            device_id=(e, (s + h) % n_seg),
            device_id_type=MESH,
        )

    def left_copy(level, h):
        return pltpu.make_async_remote_copy(
            src_ref=outbox.at[level, pl.ds(1, 3)],
            dst_ref=from_right.at[level],
            send_sem=left_send.at[level],
            recv_sem=right_recv.at[level],
            device_id=(e, (s + n_seg - h) % n_seg),
            device_id_type=MESH,
        )

    def start_left(level, h):
        @pl.when(s >= h)
        def _():
            left_copy(level, h).start()

    def start_right(level, h):
        @pl.when(s + h < n_seg)
        def _():
            right_copy(level, h).start()

    def await_right(level, h):
        @pl.when(s + h < n_seg)
        def _():
            left_copy(level, h).wait_recv()

    def await_left(level, h):
        @pl.when(s >= h)
        def _():
            right_copy(level, h).wait_recv()

    start_left(0, 1)
    here = jnp.full((BS, WIDE), s, jnp.int32)

    def interior_factors():
        ((cl1,), (cr1,)) = products([ul1, l32], [g1])
        ((w0g0,), (v1g0,)) = products([w[0], v[1]], [g0])
        ((w2g2,), (v3g2,)) = products([w[2], v[3]], [g2])
        ((p0l, p0r, p0g), (p2l, p2r, p2g)) = products([g0w1, g2v2], [b1l, b1r, g1])
        ((q0l,), (q0r,), (i0,)) = products([cl1, cr1, p0g], [v1g0])
        ((q2l,), (q2r,), (i2,)) = products([cl1, cr1, p2g], [w2g2])
        factors[0, 0], factors[1, 0], factors[2, 0] = g0v0 + p0l, b1l, jnp.where(has1, p2l, g2v2)
        factors[0, 1], factors[1, 1], factors[2, 1] = p0r, b1r, g2w3 + jnp.where(has1, p2r, 0.0)
        factors[0, 2], factors[1, 2], factors[2, 2] = w0g0 + q0l, cl1, jnp.where(has1, q2l, w2g2)
        factors[0, 3], factors[1, 3], factors[2, 3] = q0r, cr1, v3g2 + jnp.where(has1, q2r, 0.0)
        factors[0, 4], factors[1, 4], factors[2, 4] = g0 + i0, g1, g2 + jnp.where(has1, i2, 0.0)

    interior_factors()

    state[0] = sigma_left
    state[1] = u_own
    state[2] = l_own
    await_right(0, 1)
    joined = here + 1 < n_seg
    first_right = jnp.where(joined, from_right[0, 2], 0.0)
    keep[3] = first_right
    state[3] = jnp.where(joined, from_right[0, 0], 0.0)
    state[4] = jnp.where(joined, from_right[0, 1], 0.0)
    state[5] = first_right

    for level, h in enumerate(hops[:-1], 1):
        (inner,) = inverses([keep[0] - state[0] - state[5]])
        ((to_r, to_l),) = products([inner], [state[3], state[2]])
        ((add_r, l_new), (u_new, add_l)) = products([state[4], state[1]], [to_r, to_l])
        outbox[level, 0] = add_r
        outbox[level, 1] = u_new
        outbox[level, 2] = l_new
        outbox[level, 3] = add_l
        start_right(level, h)
        start_left(level, h)
        if level == 1:
            load.wait()
            for j in range(screened.shape[0]):
                for k in range(SLOTS):
                    turned[j, k] = pltpu.roll(screened[j, 0, k], BS, 1)
        await_left(level, h)
        joined = here >= h
        state[0] = state[0] + jnp.where(joined, from_left[level, 0], 0.0)
        state[1] = jnp.where(joined, from_left[level, 1], 0.0)
        state[2] = jnp.where(joined, from_left[level, 2], 0.0)
        await_right(level, h)
        joined = here + h < n_seg
        state[3] = jnp.where(joined, from_right[level, 0], 0.0)
        state[4] = jnp.where(joined, from_right[level, 1], 0.0)
        state[5] = state[5] + jnp.where(joined, from_right[level, 2], 0.0)

    lower = here < n_seg // 2
    (inner,) = inverses([keep[0] - state[0] - state[5]])
    near = product(inner, jnp.where(lower, state[3], state[2]))
    half_in[0] = product(jnp.where(lower, state[4], state[1]), near)
    half = pltpu.make_async_remote_copy(
        src_ref=half_in.at[0],
        dst_ref=half_in.at[1],
        send_sem=half_send,
        recv_sem=half_recv,
        device_id=(e, (s + n_seg // 2) % n_seg),
        device_id_type=MESH,
    )
    half.start()
    half.wait_recv()
    arrived = half_in[1]
    sigma_left = state[0] + jnp.where(lower, 0.0, arrived)
    sigma_right = state[5] + jnp.where(lower, arrived, 0.0)

    g_rep, g_end = inverses(
        [keep[0] - sigma_left - sigma_right, keep[0] - sigma_left - keep[3]]
    )
    g_out[...] = g_end
    end_copy = pltpu.make_async_remote_copy(
        src_ref=g_out,
        dst_ref=g_in,
        send_sem=g_send,
        recv_sem=g_recv,
        device_id=(e, (s + 1) % n_seg),
        device_id_type=MESH,
    )

    @pl.when(s + 1 < n_seg)
    def _():
        end_copy.start()

    far = n_z // 2
    pieces = [(SLOTS - 1, 1), (0, SLOTS - 1)]
    split = [(0, 2), (2, 2)]

    def ring_copy(way, d, piece):
        first, size = pieces[piece] if d < far else split[way]
        if way == 0:
            owner, target = (e + 2 * (n_energy - d + 1)) % n_energy, up_e
        else:
            owner, target = (e + 2 * (d - 1)) % n_energy, down_e
        block = gathered.at[owner, pl.ds(first, size)]
        return pltpu.make_async_remote_copy(
            src_ref=block,
            dst_ref=block,
            send_sem=ring_send.at[way, d - 1, piece],
            recv_sem=ring_recv.at[way, d - 1, piece],
            device_id=(target, s),
            device_id_type=MESH,
        )

    def ring_arrival(way, d, piece):
        first, size = pieces[piece] if d < far else split[way]
        owner = (e + 2 * (n_energy - d)) % n_energy if way == 0 else (e + 2 * d) % n_energy
        block = gathered.at[owner, pl.ds(first, size)]
        pltpu.make_async_remote_copy(
            src_ref=block,
            dst_ref=block,
            send_sem=ring_send.at[way, d - 1, piece],
            recv_sem=ring_recv.at[way, d - 1, piece],
            device_id=(up_e if way == 0 else down_e, s),
            device_id_type=MESH,
        ).wait_recv()

    def pair_copy(way, d, piece, arriving=False):
        first, size = pieces[piece] if d < far else split[way]
        base = pair_e if arriving else e
        owner = (base + 2 * (n_energy - d)) % n_energy if way == 0 else (base + 2 * d) % n_energy
        block = gathered.at[owner, pl.ds(first, size)]
        return pltpu.make_async_remote_copy(
            src_ref=block,
            dst_ref=block,
            send_sem=pair_send.at[way, d, piece],
            recv_sem=pair_recv.at[way, d, piece],
            device_id=(pair_e, s),
            device_id_type=MESH,
        )

    def start_own(piece):
        for way in range(2):
            if far > 1:
                ring_copy(way, 1, piece).start()
        pair_copy(0, 0, piece).start()

    gathered[e, SLOTS - 1] = g_rep.astype(bf16)
    start_own(0)

    @pl.when(s > 0)
    def _():
        end_copy.wait_recv()

    g_left = jnp.where(here > 0, g_in[...], 0.0)
    bl = [factors[m, 0] for m in range(3)]
    cl = [factors[m, 2] for m in range(3)]
    k1 = [r[0] for r in products(bl, [g_left])]
    k2 = products([g_left], cl)[0]
    t1 = [r[0] for r in products(k1, [keep[1]])]
    t2 = products([keep[2]], k2)[0]
    direct = [product(k1[m], cl[m]) for m in range(3)]
    t3 = [r[0] for r in products([t1[m] + factors[m, 1] for m in range(3)], [g_rep])]
    for m in range(3):
        g_m = factors[m, 4] + direct[m] + product(t3[m], t2[m] + factors[m, 3])
        gathered[e, m] = g_m.astype(bf16)
    start_own(1)
    if far == 1:
        for way in range(2):
            ring_copy(way, 1, 0).start()

    for d in range(1, far):
        for piece in range(2):
            for way in range(2):
                ring_arrival(way, d, piece)
                if d + 1 < far:
                    ring_copy(way, d + 1, piece).start()
                elif piece == 1:
                    ring_copy(way, far, 0).start()
                pair_copy(way, d, piece).start()
    for way in range(2):
        ring_arrival(way, far, 0)
        pair_copy(way, far, 0).start()

    moved = [(0, 0, 0), (0, 0, 1)]
    for d in range(1, far):
        for way in range(2):
            for piece in range(2):
                ring_copy(way, d, piece).wait_send()
                moved.append((way, d, piece))
    for way in range(2):
        ring_copy(way, far, 0).wait_send()
        moved.append((way, far, 0))
    for way, d, piece in moved:
        pair_copy(way, d, piece).wait_send()
        pair_copy(way, d, piece, arriving=True).wait_recv()

    for level, h in enumerate([1] + hops[:-1]):

        @pl.when(s >= h)
        def _(level=level, h=h):
            left_copy(level, h).wait_send()

        if level > 0:

            @pl.when(s + h < n_seg)
            def _(level=level, h=h):
                right_copy(level, h).wait_send()

    half.wait_send()

    @pl.when(s + 1 < n_seg)
    def _():
        end_copy.wait_send()

    shifts = screened.shape[0]
    source = [sources[0, j] for j in range(shifts)]
    for k in range(SLOTS):
        place = jnp.minimum(SLOTS - count + k, SLOTS - 1)
        same = cross = None
        for j in range(shifts):
            g = gathered[source[j], place].astype(f32)
            one, other = g * screened[j, 0, k], g * turned[j, k]
            same = one if same is None else same + one
            cross = other if cross is None else cross + other
        value = jnp.where(lane < BS, same - pltpu.roll(same, BS, 1), cross + pltpu.roll(cross, BS, 1))
        out_ref[0, 0, k] = jnp.where(many > k, value, 0.0)


def body(n_energy, n_seg, energies, h_blocks, couplings, shift_real, shift_rate, screened, sources, counts):
    shifts = screened.shape[0]
    n_z = n_energy // 2
    far = n_z // 2
    levels = max(n_seg.bit_length() - 1, 1)
    vmem = pl.BlockSpec(memory_space=pltpu.VMEM)
    smem = pl.BlockSpec(memory_space=pltpu.SMEM)
    block = (BS, WIDE)
    dma = pltpu.SemaphoreType.DMA
    return pl.pallas_call(
        functools.partial(kernel, n_energy, n_seg),
        out_shape=jax.ShapeDtypeStruct((1, 1, SLOTS) + block, f32),
        in_specs=[smem, smem, smem, vmem, vmem, vmem, vmem, pl.BlockSpec(memory_space=pl.ANY)],
        out_specs=vmem,
        scratch_shapes=[
            pltpu.VMEM((SLOTS,) + block, f32),
            pltpu.VMEM((SLOTS,) + block, f32),
            pltpu.VMEM((SLOTS,) + block, f32),
            pltpu.VMEM((4,) + block, f32),
            pltpu.VMEM((3, 5) + block, f32),
            pltpu.VMEM((6,) + block, f32),
            pltpu.VMEM((levels, 4) + block, f32),
            pltpu.VMEM((levels, 3) + block, f32),
            pltpu.VMEM((levels, 3) + block, f32),
            pltpu.VMEM((2,) + block, f32),
            pltpu.VMEM(block, f32),
            pltpu.VMEM(block, f32),
            pltpu.VMEM((n_energy, SLOTS) + block, bf16),
            pltpu.VMEM((shifts, 1, SLOTS) + block, f32),
            pltpu.VMEM((shifts, SLOTS) + block, f32),
            dma,
            dma((levels,)),
            dma((levels,)),
            dma((levels,)),
            dma((levels,)),
            dma,
            dma,
            dma,
            dma,
            dma((2, far, 2)),
            dma((2, far, 2)),
            dma((2, far + 1, 2)),
            dma((2, far + 1, 2)),
        ],
        compiler_params=pltpu.CompilerParams(collective_id=0, has_side_effects=True),
        name="greens",
    )(counts, sources, energies, h_blocks, couplings, shift_real, shift_rate, screened)


def solution(mesh):
    in_specs = (
        P("energy"),
        P("seg", None, None, None),
        P("seg", None, None, None),
        P("energy", "seg", None),
        P("energy", "seg", None),
        P(None, "seg", None, None, None),
        P("energy", None),
        P("seg"),
    )
    out_specs = P("energy", "seg", None, None, None)
    run = functools.partial(body, mesh.shape["energy"], mesh.shape["seg"])
    return jax.shard_map(run, mesh=mesh, in_specs=in_specs, out_specs=out_specs, check_vma=False)
```

```python
import functools

import jax
import jax.numpy as jnp
from jax import lax
from jax.experimental import pallas as pl
from jax.experimental.pallas import tpu as pltpu
from jax.sharding import PartitionSpec as P

BS = 64
SLOTS = 4
WIDE = 2 * BS
broadening = 0.02
f32 = jnp.float32
bf16 = jnp.bfloat16
MESH = pl.DeviceIdType.MESH


def times_i(m):
    lane = lax.broadcasted_iota(jnp.int32, m.shape, 1)
    turned = pltpu.roll(m, BS, 1)
    return jnp.where(lane < BS, -turned, turned)


def expand(m):
    return jnp.concatenate([m, times_i(m)], 0)


def products(lefts, rights):
    left = lefts[0] if len(lefts) == 1 else jnp.concatenate(lefts, 0)
    right = [expand(m) for m in rights]
    right = right[0] if len(right) == 1 else jnp.concatenate(right, 1)
    out = jnp.dot(left, right, precision=lax.Precision.HIGHEST, preferred_element_type=f32)
    return [
        [out[BS * i : BS * i + BS, WIDE * j : WIDE * j + WIDE] for j in range(len(rights))]
        for i in range(len(lefts))
    ]


def multiply(a, wide):
    return jnp.dot(a, wide, precision=lax.Precision.HIGHEST, preferred_element_type=f32)


def product(a, b):
    return products([a], [b])[0][0]


def adjoint(m):
    t = jnp.transpose(m)
    return jnp.concatenate([t[:BS], -t[BS:]], 1)


def inverses(mats, size=BS):
    lane8 = lax.broadcasted_iota(jnp.int32, (8, WIDE), 1)
    row8 = lax.broadcasted_iota(jnp.int32, (8, WIDE), 0)
    lane = lax.broadcasted_iota(jnp.int32, (BS, WIDE), 1)
    mats = list(mats)
    for start in range(0, BS, size):
        group = (lane & (BS - 1)) // size == start // size
        blocks = range(start // 8, (start + size) // 8)
        held = [{q: m[8 * q : 8 * q + 8] for q in blocks} for m in mats]
        for p in blocks:
            own = (lane8 & (BS - 1)) // 8 == p
            for rows in held:
                mine = rows[p]
                x = jnp.where(own, jnp.where(lane8 == row8 + 8 * p, 1.0, 0.0), mine)
                z = jnp.where(own, jnp.where(lane8 == row8 + (8 * p + BS), 1.0, 0.0), times_i(mine))
                c_re = [jnp.broadcast_to(mine[:, 8 * p + k : 8 * p + k + 1], (8, WIDE)) for k in range(8)]
                c_im = [
                    jnp.broadcast_to(mine[:, BS + 8 * p + k : BS + 8 * p + k + 1], (8, WIDE))
                    for k in range(8)
                ]
                for k in range(8):
                    p_re = jnp.broadcast_to(c_re[k][k : k + 1], (8, WIDE))
                    p_im = jnp.broadcast_to(c_im[k][k : k + 1], (8, WIDE))
                    scale = 1.0 / (p_re * p_re + p_im * p_im)
                    q_re, q_im = p_re * scale, -(p_im * scale)
                    x_k = jnp.broadcast_to(x[k : k + 1], (8, WIDE))
                    z_k = jnp.broadcast_to(z[k : k + 1], (8, WIDE))
                    x_s, z_s = x_k * q_re + z_k * q_im, z_k * q_re - x_k * q_im
                    m_re, m_im = c_re[k], c_im[k]
                    pivot = row8 == k
                    for j in range(k + 1, 8):
                        r_re = jnp.broadcast_to(c_re[j][k : k + 1], (8, WIDE))
                        r_im = jnp.broadcast_to(c_im[j][k : k + 1], (8, WIDE))
                        s_re, s_im = r_re * q_re - r_im * q_im, r_re * q_im + r_im * q_re
                        c_re[j] = jnp.where(pivot, s_re, c_re[j] - (m_re * s_re - m_im * s_im))
                        c_im[j] = jnp.where(pivot, s_im, c_im[j] - (m_re * s_im + m_im * s_re))
                    x, z = (
                        jnp.where(pivot, x_s, x - (m_re * x_s + m_im * z_s)),
                        jnp.where(pivot, z_s, z - (m_re * z_s - m_im * x_s)),
                    )
                for q in blocks:
                    if q == p:
                        continue
                    total = None
                    for k in range(8):
                        n_re = jnp.broadcast_to(rows[q][:, 8 * p + k : 8 * p + k + 1], (8, WIDE))
                        n_im = jnp.broadcast_to(rows[q][:, BS + 8 * p + k : BS + 8 * p + k + 1], (8, WIDE))
                        term = n_re * x[k : k + 1] + n_im * z[k : k + 1]
                        total = term if total is None else total + term
                    rows[q] = jnp.where(own, 0.0, rows[q]) - total
                rows[p] = x
        for b, m in enumerate(mats):
            if size == BS:
                mats[b] = jnp.concatenate([held[b][q] for q in blocks], 0)
                continue
            x = jnp.concatenate([held[b][q] for q in blocks], 0)
            before = jnp.zeros((start, WIDE), f32)
            after = jnp.zeros((BS - size - start, WIDE), f32)
            right = [r for r in (before, x, after, before, times_i(x), after) if r.shape[0]]
            gone = jnp.dot(
                m, jnp.concatenate(right, 0), precision=lax.Precision.HIGHEST, preferred_element_type=f32
            )
            rest = jnp.where(group, 0.0, m) - gone
            parts = [r for r in (rest[:start], x, rest[start + size :]) if r.shape[0]]
            mats[b] = jnp.concatenate(parts, 0)
    return mats


def kernel(
    n_energy, n_seg,
    counts, sources, energies, h_ref, u_ref, real_ref, rate_ref, screened_hbm,
    out_ref,
    a_all, w_all, v_all, keep, factors, state, outbox, from_left, from_right, half_in,
    g_out, g_in, gathered, screened, turned,
    load_sem, left_send, left_recv, right_send, right_recv, half_send, half_recv,
    g_send, g_recv, ring_send, ring_recv, pair_send, pair_recv,
):
    e = lax.axis_index("energy")
    s = lax.axis_index("seg")
    n_z = n_energy // 2
    core = e % 2
    up_e = (e + 2) % n_energy
    down_e = (e + n_energy - 2) % n_energy
    pair_e = e + 1 - 2 * core

    barrier = pltpu.get_barrier_semaphore()
    hops = []
    h = 1
    while h < n_seg:
        hops.append(h)
        h *= 2
    far = n_z // 2
    leap = far // 2 if far >= 4 else n_z
    greeted = [(up_e, s), (down_e, s), (pair_e, s)]
    if leap < far:
        greeted += [((e + 2 * leap) % n_energy, s), ((e + n_energy - 2 * leap) % n_energy, s)]
    for h in hops[:-1]:
        greeted += [(e, (s + h) % n_seg), (e, (s + n_seg - h) % n_seg)]
    greeted.append((e, (s + n_seg // 2) % n_seg))
    for device in greeted:
        pl.semaphore_signal(barrier, inc=1, device_id=device, device_id_type=MESH)

    load = pltpu.make_async_copy(screened_hbm, screened, load_sem)
    load.start()

    count = counts[0]
    energy = energies[0]
    row = lax.broadcasted_iota(jnp.int32, (BS, WIDE), 0)
    lane = lax.broadcasted_iota(jnp.int32, (BS, WIDE), 1)
    diagonal = (lane & (BS - 1)) == row
    attached = jnp.where(s > 0, 1.0, 0.0).astype(f32)
    for k in range(SLOTS):
        real = energy - real_ref[0, :, BS * k : BS * k + BS]
        imag = broadening + rate_ref[0, :, BS * k : BS * k + BS]
        line = jnp.concatenate([real, imag], 1)
        a_all[k] = jnp.where(diagonal, line, 0.0) - h_ref[0, k]
        w = u_ref[0, k]
        if k == 0:
            w = w * attached
        w_all[k] = w
        v_all[k] = adjoint(w)

    slot = [jnp.maximum(count + (place - SLOTS), 0) for place in range(SLOTS)]
    a = [a_all[i] for i in slot]
    w = [w_all[i] for i in slot]
    v = [v_all[i] for i in slot]
    many = jnp.full((BS, WIDE), count, jnp.int32)
    has0, has1, has2 = many >= 4, many >= 3, many >= 2

    g0, g2 = inverses([a[0], a[2]], BS // 2)
    ((g0w1, g0v0),) = products([g0], [w[1], v[0]])
    ((g2w3, g2v2),) = products([g2], [w[3], v[2]])
    (u01, d0l), (d01, l10) = products([w[0], v[1]], [g0w1, g0v0])
    (u23, d2x), (d2r, l32) = products([w[2], v[3]], [g2w3, g2v2])
    d1 = a[1] - jnp.where(has0, d01, 0.0) - d2x
    ul1 = jnp.where(has0, u01, w[1])
    l1l = jnp.where(has0, l10, v[1])
    (g1,) = inverses([d1])
    ((b1r, b1l),) = products([g1], [u23, l1l])
    (u13, d1l), (d1r, l31) = products([ul1, l32], [b1r, b1l])
    u_own = jnp.where(has1, u13, jnp.where(has2, u23, w[3]))
    l_own = jnp.where(has1, l31, jnp.where(has2, l32, v[3]))
    sigma_left = jnp.where(has1, d1r, 0.0) + jnp.where(has2, d2r, 0.0)
    to_left = jnp.where(has0, d0l, 0.0) + jnp.where(has1, d1l, jnp.where(has2, d2x, 0.0))

    outbox[0, 1] = u_own
    outbox[0, 2] = l_own
    outbox[0, 3] = to_left
    keep[0] = a[3]
    keep[1] = u_own
    keep[2] = l_own
    pl.semaphore_wait(barrier, len(greeted))

    def right_copy(level, h, part):
        first, size = ((0, 1), (1, 2))[part]
        return pltpu.make_async_remote_copy(
            src_ref=outbox.at[level, pl.ds(first, size)],
            dst_ref=from_left.at[level, pl.ds(first, size)],
            send_sem=right_send.at[level, part],
            recv_sem=left_recv.at[level, part],
            device_id=(e, (s + h) % n_seg),
            device_id_type=MESH,
        )

    def left_copy(level, h, part):
        first, size = ((2, 1), (0, 2))[part]
        return pltpu.make_async_remote_copy(
            src_ref=outbox.at[level, pl.ds(first + 1, size)],
            dst_ref=from_right.at[level, pl.ds(first, size)],
            send_sem=left_send.at[level, part],
            recv_sem=right_recv.at[level, part],
            device_id=(e, (s + n_seg - h) % n_seg),
            device_id_type=MESH,
        )

    def start_left(level, h, part):
        @pl.when(s >= h)
        def _():
            left_copy(level, h, part).start()

    def start_right(level, h, part):
        @pl.when(s + h < n_seg)
        def _():
            right_copy(level, h, part).start()

    def await_right(level, h, part):
        @pl.when(s + h < n_seg)
        def _():
            left_copy(level, h, part).wait_recv()

    def await_left(level, h, part):
        @pl.when(s >= h)
        def _():
            right_copy(level, h, part).wait_recv()

    start_left(0, 1, 0)
    start_left(0, 1, 1)
    here = jnp.full((BS, WIDE), s, jnp.int32)

    def interior_factors():
        ((cl1,), (cr1,)) = products([ul1, l32], [g1])
        ((w0g0,), (v1g0,)) = products([w[0], v[1]], [g0])
        ((w2g2,), (v3g2,)) = products([w[2], v[3]], [g2])
        ((p0l, p0r, p0g), (p2l, p2r, p2g)) = products([g0w1, g2v2], [b1l, b1r, g1])
        ((q0l,), (q0r,), (i0,)) = products([cl1, cr1, p0g], [v1g0])
        ((q2l,), (q2r,), (i2,)) = products([cl1, cr1, p2g], [w2g2])
        factors[0, 0], factors[1, 0], factors[2, 0] = g0v0 + p0l, b1l, jnp.where(has1, p2l, g2v2)
        factors[0, 1], factors[1, 1], factors[2, 1] = p0r, b1r, g2w3 + jnp.where(has1, p2r, 0.0)
        factors[0, 2], factors[1, 2], factors[2, 2] = w0g0 + q0l, cl1, jnp.where(has1, q2l, w2g2)
        factors[0, 3], factors[1, 3], factors[2, 3] = q0r, cr1, v3g2 + jnp.where(has1, q2r, 0.0)
        factors[0, 4], factors[1, 4], factors[2, 4] = g0 + i0, g1, g2 + jnp.where(has1, i2, 0.0)

    interior_factors()

    state[0] = sigma_left
    state[1] = u_own
    state[2] = l_own
    await_right(0, 1, 0)
    first_right = jnp.where(here + 1 < n_seg, from_right[0, 2], 0.0)
    keep[3] = first_right
    state[5] = first_right

    def take_pairs(level, h):
        if level > 0:
            await_left(level, h, 1)
            joined = here >= h
            state[1] = jnp.where(joined, from_left[level, 1], 0.0)
            state[2] = jnp.where(joined, from_left[level, 2], 0.0)
        await_right(level, h, 1)
        joined = here + h < n_seg
        state[3] = jnp.where(joined, from_right[level, 0], 0.0)
        state[4] = jnp.where(joined, from_right[level, 1], 0.0)

    last = (0, 1)
    for level, h in enumerate(hops[:-1], 1):
        (inner,) = inverses([keep[0] - state[0] - state[5]])
        take_pairs(*last)
        last = (level, h)
        ((to_r, to_l),) = products([inner], [state[3], state[2]])
        wide_r, wide_l = expand(to_r), expand(to_l)
        outbox[level, 0] = multiply(state[4], wide_r)
        outbox[level, 3] = multiply(state[1], wide_l)
        start_right(level, h, 0)
        start_left(level, h, 0)
        outbox[level, 1] = multiply(state[1], wide_r)
        outbox[level, 2] = multiply(state[4], wide_l)
        start_right(level, h, 1)
        start_left(level, h, 1)
        if level == 1:
            load.wait()
            for j in range(screened.shape[0]):
                for k in range(SLOTS):
                    turned[j, k] = pltpu.roll(screened[j, 0, k], BS, 1)
        await_left(level, h, 0)
        state[0] = state[0] + jnp.where(here >= h, from_left[level, 0], 0.0)
        await_right(level, h, 0)
        state[5] = state[5] + jnp.where(here + h < n_seg, from_right[level, 2], 0.0)

    lower = here < n_seg // 2
    (inner,) = inverses([keep[0] - state[0] - state[5]])
    take_pairs(*last)
    near = product(inner, jnp.where(lower, state[3], state[2]))
    half_in[0] = product(jnp.where(lower, state[4], state[1]), near)
    half = pltpu.make_async_remote_copy(
        src_ref=half_in.at[0],
        dst_ref=half_in.at[1],
        send_sem=half_send,
        recv_sem=half_recv,
        device_id=(e, (s + n_seg // 2) % n_seg),
        device_id_type=MESH,
    )
    half.start()
    half.wait_recv()
    arrived = half_in[1]
    sigma_left = state[0] + jnp.where(lower, 0.0, arrived)
    sigma_right = state[5] + jnp.where(lower, arrived, 0.0)

    g_rep, g_end = inverses(
        [keep[0] - sigma_left - sigma_right, keep[0] - sigma_left - keep[3]], BS // 2
    )
    g_out[...] = g_end
    end_copy = pltpu.make_async_remote_copy(
        src_ref=g_out,
        dst_ref=g_in,
        send_sem=g_send,
        recv_sem=g_recv,
        device_id=(e, (s + 1) % n_seg),
        device_id_type=MESH,
    )

    @pl.when(s + 1 < n_seg)
    def _():
        end_copy.start()

    pieces = [(SLOTS - 1, 1), (0, SLOTS - 1)]
    split = [(0, 2), (2, 2)]

    def ring_copy(way, d, piece):
        first, size = pieces[piece] if d < far else split[way]
        if d == leap:
            owner = e
            target = (e + 2 * leap) % n_energy if way == 0 else (e + n_energy - 2 * leap) % n_energy
        elif way == 0:
            owner, target = (e + 2 * (n_energy - d + 1)) % n_energy, up_e
        else:
            owner, target = (e + 2 * (d - 1)) % n_energy, down_e
        block = gathered.at[owner, pl.ds(first, size)]
        return pltpu.make_async_remote_copy(
            src_ref=block,
            dst_ref=block,
            send_sem=ring_send.at[way, d - 1, piece],
            recv_sem=ring_recv.at[way, d - 1, piece],
            device_id=(target, s),
            device_id_type=MESH,
        )

    def ring_arrival(way, d, piece):
        first, size = pieces[piece] if d < far else split[way]
        owner = (e + 2 * (n_energy - d)) % n_energy if way == 0 else (e + 2 * d) % n_energy
        block = gathered.at[owner, pl.ds(first, size)]
        pltpu.make_async_remote_copy(
            src_ref=block,
            dst_ref=block,
            send_sem=ring_send.at[way, d - 1, piece],
            recv_sem=ring_recv.at[way, d - 1, piece],
            device_id=(up_e if way == 0 else down_e, s),
            device_id_type=MESH,
        ).wait_recv()

    def pair_copy(way, d, piece, arriving=False):
        first, size = pieces[piece] if d < far else split[way]
        base = pair_e if arriving else e
        owner = (base + 2 * (n_energy - d)) % n_energy if way == 0 else (base + 2 * d) % n_energy
        block = gathered.at[owner, pl.ds(first, size)]
        return pltpu.make_async_remote_copy(
            src_ref=block,
            dst_ref=block,
            send_sem=pair_send.at[way, d, piece],
            recv_sem=pair_recv.at[way, d, piece],
            device_id=(pair_e, s),
            device_id_type=MESH,
        )

    def start_own(piece):
        for way in range(2):
            if leap < far:
                ring_copy(way, leap, piece).start()
        for way in range(2):
            if far > 1:
                ring_copy(way, 1, piece).start()
        pair_copy(0, 0, piece).start()

    gathered[e, SLOTS - 1] = g_rep.astype(bf16)
    start_own(0)

    @pl.when(s > 0)
    def _():
        end_copy.wait_recv()

    g_left = jnp.where(here > 0, g_in[...], 0.0)
    bl = [factors[m, 0] for m in range(3)]
    cl = [factors[m, 2] for m in range(3)]
    k1 = [r[0] for r in products(bl, [g_left])]
    k2 = products([g_left], cl)[0]
    t1 = [r[0] for r in products(k1, [keep[1]])]
    t2 = products([keep[2]], k2)[0]
    direct = [product(k1[m], cl[m]) for m in range(3)]
    t3 = [r[0] for r in products([t1[m] + factors[m, 1] for m in range(3)], [g_rep])]
    for m in range(3):
        g_m = factors[m, 4] + direct[m] + product(t3[m], t2[m] + factors[m, 3])
        gathered[e, m] = g_m.astype(bf16)
    start_own(1)
    if far == 1:
        for way in range(2):
            ring_copy(way, 1, 0).start()

    order = list(range(1, far))
    if leap < far:
        order = sorted(set(range(1, far)), key=lambda d: d + 0.5 if d < leap else d - leap + 1.6)
    for d in order:
        for piece in range(2):
            for way in range(2):
                ring_arrival(way, d, piece)
                if d + 1 == leap:
                    pass
                elif d + 1 < far:
                    ring_copy(way, d + 1, piece).start()
                elif piece == 1:
                    ring_copy(way, far, 0).start()
                pair_copy(way, d, piece).start()
    for way in range(2):
        ring_arrival(way, far, 0)
        pair_copy(way, far, 0).start()

    moved = [(0, 0, 0), (0, 0, 1)]
    for d in range(1, far):
        for way in range(2):
            for piece in range(2):
                ring_copy(way, d, piece).wait_send()
                moved.append((way, d, piece))
    for way in range(2):
        ring_copy(way, far, 0).wait_send()
        moved.append((way, far, 0))
    for way, d, piece in moved:
        pair_copy(way, d, piece).wait_send()
        pair_copy(way, d, piece, arriving=True).wait_recv()

    for level, h in enumerate([1] + hops[:-1]):
        for part in range(2):

            @pl.when(s >= h)
            def _(level=level, h=h, part=part):
                left_copy(level, h, part).wait_send()

            if level > 0:

                @pl.when(s + h < n_seg)
                def _(level=level, h=h, part=part):
                    right_copy(level, h, part).wait_send()

    half.wait_send()

    @pl.when(s + 1 < n_seg)
    def _():
        end_copy.wait_send()

    shifts = screened.shape[0]
    source = [sources[0, j] for j in range(shifts)]
    for k in range(SLOTS):
        place = jnp.minimum(SLOTS - count + k, SLOTS - 1)
        same = cross = None
        for j in range(shifts):
            g = gathered[source[j], place].astype(f32)
            one, other = g * screened[j, 0, k], g * turned[j, k]
            same = one if same is None else same + one
            cross = other if cross is None else cross + other
        value = jnp.where(lane < BS, same - pltpu.roll(same, BS, 1), cross + pltpu.roll(cross, BS, 1))
        out_ref[0, 0, k] = jnp.where(many > k, value, 0.0)


def body(n_energy, n_seg, energies, h_blocks, couplings, shift_real, shift_rate, screened, sources, counts):
    shifts = screened.shape[0]
    n_z = n_energy // 2
    far = n_z // 2
    levels = max(n_seg.bit_length() - 1, 1)
    vmem = pl.BlockSpec(memory_space=pltpu.VMEM)
    smem = pl.BlockSpec(memory_space=pltpu.SMEM)
    block = (BS, WIDE)
    dma = pltpu.SemaphoreType.DMA
    return pl.pallas_call(
        functools.partial(kernel, n_energy, n_seg),
        out_shape=jax.ShapeDtypeStruct((1, 1, SLOTS) + block, f32),
        in_specs=[smem, smem, smem, vmem, vmem, vmem, vmem, pl.BlockSpec(memory_space=pl.ANY)],
        out_specs=vmem,
        scratch_shapes=[
            pltpu.VMEM((SLOTS,) + block, f32),
            pltpu.VMEM((SLOTS,) + block, f32),
            pltpu.VMEM((SLOTS,) + block, f32),
            pltpu.VMEM((4,) + block, f32),
            pltpu.VMEM((3, 5) + block, f32),
            pltpu.VMEM((6,) + block, f32),
            pltpu.VMEM((levels, 4) + block, f32),
            pltpu.VMEM((levels, 3) + block, f32),
            pltpu.VMEM((levels, 3) + block, f32),
            pltpu.VMEM((2,) + block, f32),
            pltpu.VMEM(block, f32),
            pltpu.VMEM(block, f32),
            pltpu.VMEM((n_energy, SLOTS) + block, bf16),
            pltpu.VMEM((shifts, 1, SLOTS) + block, f32),
            pltpu.VMEM((shifts, SLOTS) + block, f32),
            dma,
            dma((levels, 2)),
            dma((levels, 2)),
            dma((levels, 2)),
            dma((levels, 2)),
            dma,
            dma,
            dma,
            dma,
            dma((2, far, 2)),
            dma((2, far, 2)),
            dma((2, far + 1, 2)),
            dma((2, far + 1, 2)),
        ],
        compiler_params=pltpu.CompilerParams(collective_id=0, has_side_effects=True),
        name="greens",
    )(counts, sources, energies, h_blocks, couplings, shift_real, shift_rate, screened)


def solution(mesh):
    in_specs = (
        P("energy"),
        P("seg", None, None, None),
        P("seg", None, None, None),
        P("energy", "seg", None),
        P("energy", "seg", None),
        P(None, "seg", None, None, None),
        P("energy", None),
        P("seg"),
    )
    out_specs = P("energy", "seg", None, None, None)
    run = functools.partial(body, mesh.shape["energy"], mesh.shape["seg"])
    return jax.shard_map(run, mesh=mesh, in_specs=in_specs, out_specs=out_specs, check_vma=False)
```

```python
import functools

import jax
import jax.numpy as jnp
from jax import lax
from jax.experimental import pallas as pl
from jax.experimental.pallas import tpu as pltpu
from jax.sharding import PartitionSpec as P

BS = 64
SLOTS = 4
WIDE = 2 * BS
broadening = 0.02
f32 = jnp.float32
bf16 = jnp.bfloat16
MESH = pl.DeviceIdType.MESH


def times_i(m):
    lane = lax.broadcasted_iota(jnp.int32, m.shape, 1)
    turned = pltpu.roll(m, BS, 1)
    return jnp.where(lane < BS, -turned, turned)


def expand(m):
    return jnp.concatenate([m, times_i(m)], 0)


def products(lefts, rights):
    left = lefts[0] if len(lefts) == 1 else jnp.concatenate(lefts, 0)
    right = [expand(m) for m in rights]
    right = right[0] if len(right) == 1 else jnp.concatenate(right, 1)
    out = jnp.dot(left, right, precision=lax.Precision.HIGHEST, preferred_element_type=f32)
    return [
        [out[BS * i : BS * i + BS, WIDE * j : WIDE * j + WIDE] for j in range(len(rights))]
        for i in range(len(lefts))
    ]


def multiply(a, wide):
    return jnp.dot(a, wide, precision=lax.Precision.HIGHEST, preferred_element_type=f32)


def product(a, b):
    return products([a], [b])[0][0]


def adjoint(m):
    t = jnp.transpose(m)
    return jnp.concatenate([t[:BS], -t[BS:]], 1)


def inverses(mats, size=BS):
    lane8 = lax.broadcasted_iota(jnp.int32, (8, WIDE), 1)
    row8 = lax.broadcasted_iota(jnp.int32, (8, WIDE), 0)
    lane = lax.broadcasted_iota(jnp.int32, (BS, WIDE), 1)
    mats = list(mats)
    for start in range(0, BS, size):
        group = (lane & (BS - 1)) // size == start // size
        blocks = range(start // 8, (start + size) // 8)
        held = [{q: m[8 * q : 8 * q + 8] for q in blocks} for m in mats]
        also = [{q: times_i(m[8 * q : 8 * q + 8]) for q in blocks} for m in mats]
        for p in blocks:
            own = (lane8 & (BS - 1)) // 8 == p
            for rows, turned in zip(held, also):
                mine = rows[p]
                x = jnp.where(own, jnp.where(lane8 == row8 + 8 * p, 1.0, 0.0), mine)
                z = jnp.where(own, jnp.where(lane8 == row8 + (8 * p + BS), 1.0, 0.0), turned[p])
                c_re = [jnp.broadcast_to(mine[:, 8 * p + k : 8 * p + k + 1], (8, WIDE)) for k in range(8)]
                c_im = [
                    jnp.broadcast_to(mine[:, BS + 8 * p + k : BS + 8 * p + k + 1], (8, WIDE))
                    for k in range(8)
                ]
                for k in range(8):
                    p_re = jnp.broadcast_to(c_re[k][k : k + 1], (8, WIDE))
                    p_im = jnp.broadcast_to(c_im[k][k : k + 1], (8, WIDE))
                    scale = 1.0 / (p_re * p_re + p_im * p_im)
                    q_re, q_im = p_re * scale, -(p_im * scale)
                    x_k = jnp.broadcast_to(x[k : k + 1], (8, WIDE))
                    z_k = jnp.broadcast_to(z[k : k + 1], (8, WIDE))
                    x_s, z_s = x_k * q_re + z_k * q_im, z_k * q_re - x_k * q_im
                    m_re, m_im = c_re[k], c_im[k]
                    pivot = row8 == k
                    for j in range(k + 1, 8):
                        r_re = jnp.broadcast_to(c_re[j][k : k + 1], (8, WIDE))
                        r_im = jnp.broadcast_to(c_im[j][k : k + 1], (8, WIDE))
                        s_re, s_im = r_re * q_re - r_im * q_im, r_re * q_im + r_im * q_re
                        c_re[j] = jnp.where(pivot, s_re, c_re[j] - (m_re * s_re - m_im * s_im))
                        c_im[j] = jnp.where(pivot, s_im, c_im[j] - (m_re * s_im + m_im * s_re))
                    x, z = (
                        jnp.where(pivot, x_s, x - (m_re * x_s + m_im * z_s)),
                        jnp.where(pivot, z_s, z - (m_re * z_s - m_im * x_s)),
                    )
                xs = [jnp.broadcast_to(x[k : k + 1], (8, WIDE)) for k in range(8)]
                zs = [jnp.broadcast_to(z[k : k + 1], (8, WIDE)) for k in range(8)]
                for q in sorted(blocks, key=lambda q: (q - p) % 8):
                    if q == p:
                        continue
                    terms = [jnp.where(own, 0.0, rows[q])]
                    others = [jnp.where(own, 0.0, turned[q])]
                    for k in range(8):
                        n_re = jnp.broadcast_to(rows[q][:, 8 * p + k : 8 * p + k + 1], (8, WIDE))
                        n_im = jnp.broadcast_to(rows[q][:, BS + 8 * p + k : BS + 8 * p + k + 1], (8, WIDE))
                        terms.append(-(n_re * xs[k] + n_im * zs[k]))
                        others.append(n_im * xs[k] - n_re * zs[k])
                    while len(terms) > 1:
                        terms = [sum(terms[n + 1 : n + 2], terms[n]) for n in range(0, len(terms), 2)]
                    while len(others) > 1:
                        others = [sum(others[n + 1 : n + 2], others[n]) for n in range(0, len(others), 2)]
                    rows[q], turned[q] = terms[0], others[0]
                rows[p] = x
        for b, m in enumerate(mats):
            if size == BS:
                mats[b] = jnp.concatenate([held[b][q] for q in blocks], 0)
                continue
            x = jnp.concatenate([held[b][q] for q in blocks], 0)
            before = jnp.zeros((start, WIDE), f32)
            after = jnp.zeros((BS - size - start, WIDE), f32)
            right = [r for r in (before, x, after, before, times_i(x), after) if r.shape[0]]
            gone = jnp.dot(
                m, jnp.concatenate(right, 0), precision=lax.Precision.HIGHEST, preferred_element_type=f32
            )
            rest = jnp.where(group, 0.0, m) - gone
            parts = [r for r in (rest[:start], x, rest[start + size :]) if r.shape[0]]
            mats[b] = jnp.concatenate(parts, 0)
    return mats


def kernel(
    n_energy, n_seg,
    counts, sources, energies, h_ref, u_ref, real_ref, rate_ref, screened_hbm,
    out_ref,
    a_all, w_all, v_all, keep, factors, state, outbox, from_left, from_right, half_in,
    g_out, g_in, gathered, screened, turned,
    load_sem, left_send, left_recv, right_send, right_recv, half_send, half_recv,
    g_send, g_recv, ring_send, ring_recv, pair_send, pair_recv,
):
    e = lax.axis_index("energy")
    s = lax.axis_index("seg")
    n_z = n_energy // 2
    core = e % 2
    up_e = (e + 2) % n_energy
    down_e = (e + n_energy - 2) % n_energy
    pair_e = e + 1 - 2 * core

    barrier = pltpu.get_barrier_semaphore()
    hops = []
    h = 1
    while h < n_seg:
        hops.append(h)
        h *= 2
    far = n_z // 2
    leap = far // 2 + 1 if far >= 4 else n_z
    greeted = [(up_e, s), (down_e, s), (pair_e, s)]
    if leap < far:
        greeted += [((e + 2 * leap) % n_energy, s), ((e + n_energy - 2 * leap) % n_energy, s)]
    for h in hops[:-1]:
        greeted += [(e, (s + h) % n_seg), (e, (s + n_seg - h) % n_seg)]
    greeted.append((e, (s + n_seg // 2) % n_seg))
    for device in greeted:
        pl.semaphore_signal(barrier, inc=1, device_id=device, device_id_type=MESH)

    load = pltpu.make_async_copy(screened_hbm, screened, load_sem)
    load.start()

    count = counts[0]
    energy = energies[0]
    row = lax.broadcasted_iota(jnp.int32, (BS, WIDE), 0)
    lane = lax.broadcasted_iota(jnp.int32, (BS, WIDE), 1)
    diagonal = (lane & (BS - 1)) == row
    attached = jnp.where(s > 0, 1.0, 0.0).astype(f32)
    for k in range(SLOTS):
        real = energy - real_ref[0, :, BS * k : BS * k + BS]
        imag = broadening + rate_ref[0, :, BS * k : BS * k + BS]
        line = jnp.concatenate([real, imag], 1)
        a_all[k] = jnp.where(diagonal, line, 0.0) - h_ref[0, k]
        w = u_ref[0, k]
        if k == 0:
            w = w * attached
        w_all[k] = w
        v_all[k] = adjoint(w)

    slot = [jnp.maximum(count + (place - SLOTS), 0) for place in range(SLOTS)]
    a = [a_all[i] for i in slot]
    w = [w_all[i] for i in slot]
    v = [v_all[i] for i in slot]
    many = jnp.full((BS, WIDE), count, jnp.int32)
    has0, has1, has2 = many >= 4, many >= 3, many >= 2

    g0, g2 = inverses([a[0], a[2]], BS // 2)
    ((g0w1, g0v0),) = products([g0], [w[1], v[0]])
    ((g2w3, g2v2),) = products([g2], [w[3], v[2]])
    (u01, d0l), (d01, l10) = products([w[0], v[1]], [g0w1, g0v0])
    (u23, d2x), (d2r, l32) = products([w[2], v[3]], [g2w3, g2v2])
    d1 = a[1] - jnp.where(has0, d01, 0.0) - d2x
    ul1 = jnp.where(has0, u01, w[1])
    l1l = jnp.where(has0, l10, v[1])
    (g1,) = inverses([d1])
    ((b1r, b1l),) = products([g1], [u23, l1l])
    (u13, d1l), (d1r, l31) = products([ul1, l32], [b1r, b1l])
    u_own = jnp.where(has1, u13, jnp.where(has2, u23, w[3]))
    l_own = jnp.where(has1, l31, jnp.where(has2, l32, v[3]))
    sigma_left = jnp.where(has1, d1r, 0.0) + jnp.where(has2, d2r, 0.0)
    to_left = jnp.where(has0, d0l, 0.0) + jnp.where(has1, d1l, jnp.where(has2, d2x, 0.0))

    outbox[0, 1] = u_own
    outbox[0, 2] = l_own
    outbox[0, 3] = to_left
    keep[0] = a[3]
    keep[1] = u_own
    keep[2] = l_own
    pl.semaphore_wait(barrier, len(greeted))

    def right_copy(level, h, part):
        first, size = ((0, 1), (1, 2))[part]
        return pltpu.make_async_remote_copy(
            src_ref=outbox.at[level, pl.ds(first, size)],
            dst_ref=from_left.at[level, pl.ds(first, size)],
            send_sem=right_send.at[level, part],
            recv_sem=left_recv.at[level, part],
            device_id=(e, (s + h) % n_seg),
            device_id_type=MESH,
        )

    def left_copy(level, h, part):
        first, size = ((2, 1), (0, 2))[part]
        return pltpu.make_async_remote_copy(
            src_ref=outbox.at[level, pl.ds(first + 1, size)],
            dst_ref=from_right.at[level, pl.ds(first, size)],
            send_sem=left_send.at[level, part],
            recv_sem=right_recv.at[level, part],
            device_id=(e, (s + n_seg - h) % n_seg),
            device_id_type=MESH,
        )

    def start_left(level, h, part):
        @pl.when(s >= h)
        def _():
            left_copy(level, h, part).start()

    def start_right(level, h, part):
        @pl.when(s + h < n_seg)
        def _():
            right_copy(level, h, part).start()

    def await_right(level, h, part):
        @pl.when(s + h < n_seg)
        def _():
            left_copy(level, h, part).wait_recv()

    def await_left(level, h, part):
        @pl.when(s >= h)
        def _():
            right_copy(level, h, part).wait_recv()

    start_left(0, 1, 0)
    start_left(0, 1, 1)
    here = jnp.full((BS, WIDE), s, jnp.int32)

    def interior_factors():
        ((cl1,), (cr1,)) = products([ul1, l32], [g1])
        ((w0g0,), (v1g0,)) = products([w[0], v[1]], [g0])
        ((w2g2,), (v3g2,)) = products([w[2], v[3]], [g2])
        ((p0l, p0r, p0g), (p2l, p2r, p2g)) = products([g0w1, g2v2], [b1l, b1r, g1])
        ((q0l,), (q0r,), (i0,)) = products([cl1, cr1, p0g], [v1g0])
        ((q2l,), (q2r,), (i2,)) = products([cl1, cr1, p2g], [w2g2])
        factors[0, 0], factors[1, 0], factors[2, 0] = g0v0 + p0l, b1l, jnp.where(has1, p2l, g2v2)
        factors[0, 1], factors[1, 1], factors[2, 1] = p0r, b1r, g2w3 + jnp.where(has1, p2r, 0.0)
        factors[0, 2], factors[1, 2], factors[2, 2] = w0g0 + q0l, cl1, jnp.where(has1, q2l, w2g2)
        factors[0, 3], factors[1, 3], factors[2, 3] = q0r, cr1, v3g2 + jnp.where(has1, q2r, 0.0)
        factors[0, 4], factors[1, 4], factors[2, 4] = g0 + i0, g1, g2 + jnp.where(has1, i2, 0.0)

    interior_factors()

    state[0] = sigma_left
    state[1] = u_own
    state[2] = l_own
    await_right(0, 1, 0)
    first_right = jnp.where(here + 1 < n_seg, from_right[0, 2], 0.0)
    keep[3] = first_right
    state[5] = first_right

    def take_pairs(level, h):
        if level > 0:
            await_left(level, h, 1)
            joined = here >= h
            state[1] = jnp.where(joined, from_left[level, 1], 0.0)
            state[2] = jnp.where(joined, from_left[level, 2], 0.0)
        await_right(level, h, 1)
        joined = here + h < n_seg
        state[3] = jnp.where(joined, from_right[level, 0], 0.0)
        state[4] = jnp.where(joined, from_right[level, 1], 0.0)

    last = (0, 1)
    for level, h in enumerate(hops[:-1], 1):
        (inner,) = inverses([keep[0] - state[0] - state[5]])
        take_pairs(*last)
        last = (level, h)
        ((to_r, to_l),) = products([inner], [state[3], state[2]])
        wide_r, wide_l = expand(to_r), expand(to_l)
        outbox[level, 0] = multiply(state[4], wide_r)
        outbox[level, 3] = multiply(state[1], wide_l)
        start_right(level, h, 0)
        start_left(level, h, 0)
        outbox[level, 1] = multiply(state[1], wide_r)
        outbox[level, 2] = multiply(state[4], wide_l)
        start_right(level, h, 1)
        start_left(level, h, 1)
        if level == 1:
            load.wait()
            for j in range(screened.shape[0]):
                for k in range(SLOTS):
                    turned[j, k] = pltpu.roll(screened[j, 0, k], BS, 1)
        await_left(level, h, 0)
        state[0] = state[0] + jnp.where(here >= h, from_left[level, 0], 0.0)
        await_right(level, h, 0)
        state[5] = state[5] + jnp.where(here + h < n_seg, from_right[level, 2], 0.0)

    lower = here < n_seg // 2
    (inner,) = inverses([keep[0] - state[0] - state[5]])
    take_pairs(*last)
    near = product(inner, jnp.where(lower, state[3], state[2]))
    half_in[0] = product(jnp.where(lower, state[4], state[1]), near)
    half = pltpu.make_async_remote_copy(
        src_ref=half_in.at[0],
        dst_ref=half_in.at[1],
        send_sem=half_send,
        recv_sem=half_recv,
        device_id=(e, (s + n_seg // 2) % n_seg),
        device_id_type=MESH,
    )
    half.start()
    half.wait_recv()
    arrived = half_in[1]
    sigma_left = state[0] + jnp.where(lower, 0.0, arrived)
    sigma_right = state[5] + jnp.where(lower, arrived, 0.0)

    g_rep, g_end = inverses(
        [keep[0] - sigma_left - sigma_right, keep[0] - sigma_left - keep[3]], BS // 2
    )
    g_out[...] = g_end
    end_copy = pltpu.make_async_remote_copy(
        src_ref=g_out,
        dst_ref=g_in,
        send_sem=g_send,
        recv_sem=g_recv,
        device_id=(e, (s + 1) % n_seg),
        device_id_type=MESH,
    )

    @pl.when(s + 1 < n_seg)
    def _():
        end_copy.start()

    pieces = [(SLOTS - 1, 1), (0, SLOTS - 1)]
    split = [(0, 2), (2, 2)]

    def ring_copy(way, d, piece):
        first, size = pieces[piece] if d < far else split[way]
        if d == leap:
            owner = e
            target = (e + 2 * leap) % n_energy if way == 0 else (e + n_energy - 2 * leap) % n_energy
        elif way == 0:
            owner, target = (e + 2 * (n_energy - d + 1)) % n_energy, up_e
        else:
            owner, target = (e + 2 * (d - 1)) % n_energy, down_e
        block = gathered.at[owner, pl.ds(first, size)]
        return pltpu.make_async_remote_copy(
            src_ref=block,
            dst_ref=block,
            send_sem=ring_send.at[way, d - 1, piece],
            recv_sem=ring_recv.at[way, d - 1, piece],
            device_id=(target, s),
            device_id_type=MESH,
        )

    def ring_arrival(way, d, piece):
        first, size = pieces[piece] if d < far else split[way]
        owner = (e + 2 * (n_energy - d)) % n_energy if way == 0 else (e + 2 * d) % n_energy
        block = gathered.at[owner, pl.ds(first, size)]
        pltpu.make_async_remote_copy(
            src_ref=block,
            dst_ref=block,
            send_sem=ring_send.at[way, d - 1, piece],
            recv_sem=ring_recv.at[way, d - 1, piece],
            device_id=(up_e if way == 0 else down_e, s),
            device_id_type=MESH,
        ).wait_recv()

    def pair_copy(way, d, piece, arriving=False):
        first, size = pieces[piece] if d < far else split[way]
        base = pair_e if arriving else e
        owner = (base + 2 * (n_energy - d)) % n_energy if way == 0 else (base + 2 * d) % n_energy
        block = gathered.at[owner, pl.ds(first, size)]
        return pltpu.make_async_remote_copy(
            src_ref=block,
            dst_ref=block,
            send_sem=pair_send.at[way, d, piece],
            recv_sem=pair_recv.at[way, d, piece],
            device_id=(pair_e, s),
            device_id_type=MESH,
        )

    def start_own(piece):
        for way in range(2):
            if leap < far:
                ring_copy(way, leap, piece).start()
        for way in range(2):
            if far > 1:
                ring_copy(way, 1, piece).start()
        pair_copy(0, 0, piece).start()

    gathered[e, SLOTS - 1] = g_rep.astype(bf16)
    start_own(0)

    @pl.when(s > 0)
    def _():
        end_copy.wait_recv()

    g_left = jnp.where(here > 0, g_in[...], 0.0)
    bl = [factors[m, 0] for m in range(3)]
    cl = [factors[m, 2] for m in range(3)]
    k1 = [r[0] for r in products(bl, [g_left])]
    k2 = products([g_left], cl)[0]
    t1 = [r[0] for r in products(k1, [keep[1]])]
    t2 = products([keep[2]], k2)[0]
    direct = [product(k1[m], cl[m]) for m in range(3)]
    t3 = [r[0] for r in products([t1[m] + factors[m, 1] for m in range(3)], [g_rep])]
    for m in range(3):
        g_m = factors[m, 4] + direct[m] + product(t3[m], t2[m] + factors[m, 3])
        gathered[e, m] = g_m.astype(bf16)
    start_own(1)
    if far == 1:
        for way in range(2):
            ring_copy(way, 1, 0).start()

    order = list(range(1, far))
    if leap < far:
        order = sorted(set(range(1, far)), key=lambda d: d + 0.5 if d < leap else d - leap + 1.6)
    for d in order:
        for piece in range(2):
            for way in range(2):
                ring_arrival(way, d, piece)
                if d + 1 == leap:
                    pass
                elif d + 1 < far:
                    ring_copy(way, d + 1, piece).start()
                elif piece == 1:
                    ring_copy(way, far, 0).start()
                pair_copy(way, d, piece).start()
    for way in range(2):
        ring_arrival(way, far, 0)
        pair_copy(way, far, 0).start()

    moved = [(0, 0, 0), (0, 0, 1)]
    for d in range(1, far):
        for way in range(2):
            for piece in range(2):
                ring_copy(way, d, piece).wait_send()
                moved.append((way, d, piece))
    for way in range(2):
        ring_copy(way, far, 0).wait_send()
        moved.append((way, far, 0))
    for way, d, piece in moved:
        pair_copy(way, d, piece).wait_send()
        pair_copy(way, d, piece, arriving=True).wait_recv()

    for level, h in enumerate([1] + hops[:-1]):
        for part in range(2):

            @pl.when(s >= h)
            def _(level=level, h=h, part=part):
                left_copy(level, h, part).wait_send()

            if level > 0:

                @pl.when(s + h < n_seg)
                def _(level=level, h=h, part=part):
                    right_copy(level, h, part).wait_send()

    half.wait_send()

    @pl.when(s + 1 < n_seg)
    def _():
        end_copy.wait_send()

    shifts = screened.shape[0]
    source = [sources[0, j] for j in range(shifts)]
    for k in range(SLOTS):
        place = jnp.minimum(SLOTS - count + k, SLOTS - 1)
        same = cross = None
        for j in range(shifts):
            g = gathered[source[j], place].astype(f32)
            one, other = g * screened[j, 0, k], g * turned[j, k]
            same = one if same is None else same + one
            cross = other if cross is None else cross + other
        value = jnp.where(lane < BS, same - pltpu.roll(same, BS, 1), cross + pltpu.roll(cross, BS, 1))
        out_ref[0, 0, k] = jnp.where(many > k, value, 0.0)


def body(n_energy, n_seg, energies, h_blocks, couplings, shift_real, shift_rate, screened, sources, counts):
    shifts = screened.shape[0]
    n_z = n_energy // 2
    far = n_z // 2
    levels = max(n_seg.bit_length() - 1, 1)
    vmem = pl.BlockSpec(memory_space=pltpu.VMEM)
    smem = pl.BlockSpec(memory_space=pltpu.SMEM)
    block = (BS, WIDE)
    dma = pltpu.SemaphoreType.DMA
    return pl.pallas_call(
        functools.partial(kernel, n_energy, n_seg),
        out_shape=jax.ShapeDtypeStruct((1, 1, SLOTS) + block, f32),
        in_specs=[smem, smem, smem, vmem, vmem, vmem, vmem, pl.BlockSpec(memory_space=pl.ANY)],
        out_specs=vmem,
        scratch_shapes=[
            pltpu.VMEM((SLOTS,) + block, f32),
            pltpu.VMEM((SLOTS,) + block, f32),
            pltpu.VMEM((SLOTS,) + block, f32),
            pltpu.VMEM((4,) + block, f32),
            pltpu.VMEM((3, 5) + block, f32),
            pltpu.VMEM((6,) + block, f32),
            pltpu.VMEM((levels, 4) + block, f32),
            pltpu.VMEM((levels, 3) + block, f32),
            pltpu.VMEM((levels, 3) + block, f32),
            pltpu.VMEM((2,) + block, f32),
            pltpu.VMEM(block, f32),
            pltpu.VMEM(block, f32),
            pltpu.VMEM((n_energy, SLOTS) + block, bf16),
            pltpu.VMEM((shifts, 1, SLOTS) + block, f32),
            pltpu.VMEM((shifts, SLOTS) + block, f32),
            dma,
            dma((levels, 2)),
            dma((levels, 2)),
            dma((levels, 2)),
            dma((levels, 2)),
            dma,
            dma,
            dma,
            dma,
            dma((2, far, 2)),
            dma((2, far, 2)),
            dma((2, far + 1, 2)),
            dma((2, far + 1, 2)),
        ],
        compiler_params=pltpu.CompilerParams(collective_id=0, has_side_effects=True),
        name="greens",
    )(counts, sources, energies, h_blocks, couplings, shift_real, shift_rate, screened)


def solution(mesh):
    in_specs = (
        P("energy"),
        P("seg", None, None, None),
        P("seg", None, None, None),
        P("energy", "seg", None),
        P("energy", "seg", None),
        P(None, "seg", None, None, None),
        P("energy", None),
        P("seg"),
    )
    out_specs = P("energy", "seg", None, None, None)
    run = functools.partial(body, mesh.shape["energy"], mesh.shape["seg"])
    return jax.shard_map(run, mesh=mesh, in_specs=in_specs, out_specs=out_specs, check_vma=False)
```
